32 devices in a mesh: wide: 16 (over z, y, core), narrow: 2 (over x).
Axes of the slice: x: 2, y: 2, z: 4, core: 2. Of those that a mesh axis runs over, the one named last changes fastest.
Arguments:
- query_values: bfloat16 [224, 1024], P('wide'), may hold values from -64 to 64
- query_scales: float32 [224, 32], P('wide'), may hold values from 0.2 to 4.5
- reference_rows: bfloat16 [3072, 1024], P(('wide', 'narrow')), may hold values from -12 to 12
Outputs:
- row_match: bfloat16 [224, 1024], P('wide')
- column_match: bfloat16 [3072, 1024], P(('wide', 'narrow'))
The draws below stay inside these ranges and needn't reach their ends.
All inputs are finite; a program needn't handle non-finite values.
Results may differ from the reference program's by a relative error of at most 0.01195.
Values may be sent and summed in bfloat16 or wider, within the bound.
A program may use at most 64 MiB of HBM per device.

```python
import math
import jax
import jax.numpy as jnp
from jax import lax

D = 1024
GROUP = 32
REF_DEV = 96
NQ = 224
NR = 3072


def build_all(key):
    base = jax.random.fold_in(key, 41)
    keys = jax.random.split(base, 6)
    ref_scale = jnp.exp(jax.random.uniform(keys[0], (NR,), jnp.float32, jnp.log(0.4), jnp.log(4.0)))
    refs = jax.random.normal(keys[2], (NR, D), jnp.float32) * ref_scale[:, None]
    row_part = jnp.exp(jax.random.uniform(keys[3], (NQ,), jnp.float32, jnp.log(0.3), jnp.log(3.0)))
    group_part = jnp.exp(jax.random.uniform(keys[4], (NQ, D // GROUP), jnp.float32, jnp.log(0.7), jnp.log(1.4)))
    scales = row_part[:, None] * group_part
    expanded = jnp.repeat(scales, GROUP, axis=1)
    queries = jnp.clip(jax.random.normal(keys[5], (NQ, D), jnp.float32), -6.0, 6.0) * expanded
    refs = jnp.clip(refs, -12.0, 12.0)
    values = jnp.clip(queries / expanded, -64.0, 64.0)
    return (values, scales, refs)


def draw_query_values(key, part):
    return build_all(key)[0].astype(jnp.bfloat16)


def draw_query_scales(key, part):
    return build_all(key)[1].astype(jnp.float32)


def draw_reference_rows(key, part):
    return build_all(key)[2].astype(jnp.bfloat16)


def setup_inputs(seed: int = 0) -> dict:
    key_of = jax.random.split(jax.random.key(seed), 4)
    return {
        "query_values": draw_query_values(jax.random.fold_in(key_of[3], 71), 0),
        "query_scales": draw_query_scales(jax.random.fold_in(key_of[3], 71), 0),
        "reference_rows": draw_reference_rows(jax.random.fold_in(key_of[3], 71), 0),
    }


def dequantize(values, scales):
    rows, width = values.shape
    groups = scales.shape[1]
    spread = values.astype(jnp.float32).reshape(rows, groups, width // groups) * scales[:, :, None]
    return spread.reshape(rows, width).astype(jnp.bfloat16)

def reference(query_values, query_scales, reference_rows):
    queries = dequantize(query_values, query_scales)
    factor = 1.0 / math.sqrt(D)
    blocks = reference_rows.reshape(NR // REF_DEV, REF_DEV, D)

    def scan_block(carry, block):
        row_max, row_sum, row_acc = carry
        scores = lax.dot_general(queries, block, (((1,), (1,)), ((), ())), preferred_element_type=jnp.float32) * factor
        fresh = jnp.maximum(row_max, lax.optimization_barrier(jnp.max(scores, axis=1)))
        shrink = jnp.exp(row_max - fresh)
        weights = jnp.exp(scores - fresh[:, None])
        row_sum = row_sum * shrink + lax.optimization_barrier(jnp.sum(weights, axis=1))
        row_acc = row_acc * shrink[:, None] + jnp.dot(weights.astype(jnp.bfloat16), block, preferred_element_type=jnp.float32)
        col_max = lax.optimization_barrier(jnp.max(scores, axis=0))
        col_exp = jnp.exp(scores - col_max[None, :])
        col_sum = lax.optimization_barrier(jnp.sum(col_exp, axis=0))
        col_acc = lax.dot_general(col_exp.astype(jnp.bfloat16), queries, (((0,), (0,)), ((), ())), preferred_element_type=jnp.float32)
        return ((fresh, row_sum, row_acc), (col_acc / col_sum[:, None]).astype(jnp.bfloat16))
    start = (jnp.full((NQ,), -jnp.inf, jnp.float32), jnp.zeros((NQ,), jnp.float32), jnp.zeros((NQ, D), jnp.float32))
    (row_max, row_sum, row_acc), columns = lax.scan(scan_block, start, blocks)
    row_match = (row_acc / row_sum[:, None]).astype(jnp.bfloat16)
    return (row_match, columns.reshape(NR, D))
```

```python
import functools
import math

import jax
import jax.numpy as jnp
from jax import lax
from jax.experimental import pallas as pl
from jax.experimental.pallas import tpu as pltpu
from jax.sharding import PartitionSpec as P

MESH = pl.DeviceIdType.MESH
LANES = 128
LIMIT = 40 << 20
F32 = jnp.float32
BF16 = jnp.bfloat16


def split3(x):
    hi = x.astype(BF16).astype(F32)
    mid = (x - hi).astype(BF16).astype(F32)
    return hi, mid, x - hi - mid


def pack_stats(top, total):
    rows = top.shape[0]
    lane = lax.broadcasted_iota(jnp.int32, (rows, LANES), 1)
    out = jnp.zeros((rows, LANES), F32)
    for i, term in enumerate(split3(top) + split3(total)):
        out = jnp.where(lane == i, term, out)
    return out.astype(BF16)


def unpack(message, width):
    t = message[:, width:].astype(F32)
    top = t[:, 0:1] + t[:, 1:2] + t[:, 2:3]
    total = t[:, 3:4] + t[:, 4:5] + t[:, 5:6]
    return message[:, :width].astype(F32), top, total


def merge(parts):
    top = functools.reduce(jnp.maximum, [p[1] for p in parts])
    acc, total = None, None
    for p in parts:
        shrink = jnp.exp(p[1] - top)
        a, s = p[0] * shrink, p[2] * shrink
        acc, total = (a, s) if acc is None else (acc + a, total + s)
    return acc, top, total


def kernel(
    dims, rows,
    values_hbm, scales_hbm, refs_hbm, row_out, col_out,
    values_ref, scales_ref, refs, q, part, stat_m, stat_s, out_c, in_c, out_y, in_y, out_z, in_z, all_x,
    out_k, in_k, result,
    load_sem, ref_sem, gz_s, gz_r, gy_s, gy_r, gc_s, gc_r,
    rc_s, rc_r, ry_s, ry_r, rz_s, rz_r, rg_s, rg_r, x_s, x_r,
):
    A, B, N = dims
    H, G = A * B, N // 2
    pad, width = q.shape[1], q.shape[2]
    count = refs.shape[1]
    factor = 1.0 / math.sqrt(width)
    w = lax.axis_index("wide")
    n = lax.axis_index("narrow")
    a, b, c = w // (B * 2), (w // 2) % B, w % 2
    g, p = n // 2, n % 2
    active = c == p
    other = 1 - p

    zdev = [{"wide": (((a + i) % A) * B + b) * 2 + c} for i in range(A)]
    ydev = [{"wide": (a * B + (b + j) % B) * 2 + c} for j in range(B)]
    cdev = {"wide": (a * B + b) * 2 + 1 - c}
    xdev = {"narrow": g * 2 + other}
    gdev = [{"narrow": ((g + k) % G) * 2 + p} for k in range(G)]
    back = {
        (i, j): ((a + A - i) % A) * B + (b + B - j) % B for i in range(A) for j in range(B)
    }
    ahead = {(i, j): ((a + i) % A) * B + (b + j) % B for i in range(A) for j in range(B)}
    gback = [(g + G - k) % G for k in range(G)]

    load_values = pltpu.make_async_copy(values_hbm, values_ref, load_sem.at[0])
    load_scales = pltpu.make_async_copy(scales_hbm, scales_ref, load_sem.at[1])
    load = pltpu.make_async_copy(refs_hbm, refs.at[p], ref_sem)
    load_values.start()
    load_scales.start()
    load.start()

    barrier = pltpu.get_barrier_semaphore()
    near = [cdev, xdev]
    far = zdev[1:] + ydev[1:] + gdev[1:]
    for d in near:
        pl.semaphore_signal(barrier, inc=1, device_id=d, device_id_type=MESH)

    @pl.when(active)
    def _():
        for d in far:
            pl.semaphore_signal(barrier, inc=1, device_id=d, device_id_type=MESH)

    load_values.wait()
    load_scales.wait()

    @pl.when(active)
    def _():

        groups = scales_ref.shape[1]
        lane = lax.broadcasted_iota(jnp.int32, (groups, width), 1)
        group = lax.broadcasted_iota(jnp.int32, (groups, width), 0)
        spread = jnp.where(lane // (width // groups) == group, 1.0, 0.0).astype(F32)
        scale = jnp.dot(
            scales_ref[...], spread, preferred_element_type=F32, precision=lax.Precision.HIGHEST
        )
        mine = values_ref[...].astype(F32) * scale
        if pad > rows:
            mine = jnp.concatenate([mine, jnp.zeros((pad - rows, width), F32)], axis=0)
        q[back[0, 0]] = mine.astype(BF16)

    load.wait()
    pl.semaphore_wait(barrier, jnp.where(active, len(near) + len(far), len(near)))

    def view(x):
        return x[0].at[x[1]] if isinstance(x, tuple) else x

    def remote(src, dst, s, r, device):
        return pltpu.make_async_remote_copy(
            src_ref=view(src), dst_ref=view(dst), send_sem=view(s), recv_sem=view(r),
            device_id=device, device_id_type=MESH,
        )

    sent = {True: [], False: [], None: []}

    def send(who, *args):
        remote(*args).start()
        sent[who].append(args)

    def arrive(dst, s, r):
        remote(dst, dst, s, r, xdev).wait_recv()

    send(None, (refs, p), (refs, p), (x_s, 0), (x_r, 0), xdev)

    def slot(i, j):
        return q, back[i, j]

    def to_core(i, j):
        e = i * B + j
        send(True, slot(i, j), slot(i, j), (gc_s, e), (gc_r, e), cdev)

    def to_y(i):
        for j in range(1, B):
            e = i * B + j
            send(True, slot(i, 0), slot(i, 0), (gy_s, e), (gy_r, e), ydev[j])

    @pl.when(active)
    def _():
        for i in reversed(range(1, A)):
            send(True, slot(0, 0), slot(0, 0), (gz_s, i), (gz_r, i), zdev[i])
        to_y(0)
        to_core(0, 0)
        for i in range(1, A):
            arrive(slot(i, 0), (gz_s, i), (gz_r, i))
            to_y(i)
            to_core(i, 0)
        for i in range(A):
            for j in range(1, B):
                e = i * B + j
                arrive(slot(i, j), (gy_s, e), (gy_r, e))
                to_core(i, j)

    @pl.when(jnp.logical_not(active))
    def _():
        for i in range(A):
            for j in range(B):
                e = i * B + j
                arrive(slot(i, j), (gc_s, e), (gc_r, e))

    arrive((refs, other), (x_s, 0), (x_r, 0))

    both = refs[...].reshape(2 * count, width)
    chunk = H
    while chunk * pad > 512 and chunk % 2 == 0:
        chunk //= 2
    for start in range(0, H, chunk):
        block = q[start : start + chunk].reshape(chunk * pad, width)
        scores = (
            lax.dot_general(block, both, (((1,), (1,)), ((), ())), preferred_element_type=F32)
            * factor
        )
        top = jnp.max(scores, axis=1, keepdims=True)
        weights = jnp.exp(scores - top)
        total = jnp.sum(weights, axis=1, keepdims=True)
        acc = jnp.dot(weights.astype(BF16), both, preferred_element_type=F32)
        part[start : start + chunk] = acc.reshape(chunk, pad, width)
        stat_m[start : start + chunk] = jnp.broadcast_to(top, (chunk * pad, LANES)).reshape(
            chunk, pad, LANES
        )
        stat_s[start : start + chunk] = jnp.broadcast_to(total, (chunk * pad, LANES)).reshape(
            chunk, pad, LANES
        )

    def own(index):
        return part[index], stat_m[index][:, 0:1], stat_s[index][:, 0:1]

    def keep(index, t):
        part[index] = t[0]
        stat_m[index] = jnp.broadcast_to(t[1], (pad, LANES))
        stat_s[index] = jnp.broadcast_to(t[2], (pad, LANES))

    def put(dst, t):
        dst[:, :width] = t[0].astype(BF16)
        dst[:, width:] = pack_stats(t[1], t[2])

    order = [(i, j) for j in reversed(range(B)) for i in reversed(range(A))]

    @pl.when(jnp.logical_not(active))
    def _():
        for i, j in order:
            e = i * B + j
            put(out_c.at[e], own(ahead[i, j]))
            send(False, (out_c, e), (in_c, e), (rc_s, e), (rc_r, e), cdev)

    every = q[...].reshape(H * pad, width)

    def columns(block):
        scores = (
            lax.dot_general(block, every, (((1,), (1,)), ((), ())), preferred_element_type=F32)
            * factor
        )
        if pad > rows:
            column = lax.broadcasted_iota(jnp.int32, scores.shape, 1)
            scores = jnp.where(column % pad < rows, scores, -jnp.inf)
        top = jnp.max(scores, axis=1, keepdims=True)
        weights = jnp.exp(scores - top)
        total = jnp.sum(weights, axis=1, keepdims=True)
        return jnp.dot(weights.astype(BF16), every, preferred_element_type=F32), top, total

    put(out_k, columns(refs[other]))
    send(None, out_k, in_k, (x_s, 1), (x_r, 1), xdev)

    @pl.when(active)
    def _():
        for i, j in order:
            e = i * B + j
            arrive((in_c, e), (rc_s, e), (rc_r, e))
            t = merge([own(ahead[i, j]), unpack(in_c[e], width)])
            if j:
                put(out_y.at[e], t)
                send(True, (out_y, e), (in_y, e), (ry_s, e), (ry_r, e), ydev[j])
            else:
                keep(ahead[i, 0], t)
        for i in reversed(range(A)):
            parts = [own(ahead[i, 0])]
            for j in range(1, B):
                e = i * B + j
                arrive((in_y, e), (ry_s, e), (ry_r, e))
                parts.append(unpack(in_y[e], width))
            t = merge(parts)
            if i:
                put(out_z.at[i], t)
                send(True, (out_z, i), (in_z, i), (rz_s, i), (rz_r, i), zdev[i])
            else:
                keep(ahead[0, 0], t)

    mine_t = columns(refs[p])

    @pl.when(active)
    def _():
        parts = [own(ahead[0, 0])]
        for i in range(1, A):
            arrive((in_z, i), (rz_s, i), (rz_r, i))
            parts.append(unpack(in_z[i], width))
        t = merge(parts)
        if G > 1:
            put(all_x.at[g], t)
            for k in range(1, G):
                send(True, (all_x, g), (all_x, g), (rg_s, k), (rg_r, k), gdev[k])
            for k in range(1, G):
                arrive((all_x, gback[k]), (rg_s, k), (rg_r, k))
            t = merge([unpack(all_x[i], width) for i in range(G)])
        result[...] = (t[0] / t[2]).astype(BF16)
        send(True, result, result, (x_s, 2), (x_r, 2), xdev)

    arrive(in_k, (x_s, 1), (x_r, 1))
    acc, _, total = merge([mine_t, unpack(in_k[...], width)])
    col_out[...] = (acc / total).astype(BF16)

    @pl.when(jnp.logical_not(active))
    def _():
        arrive(result, (x_s, 2), (x_r, 2))

    row_out[...] = result[...][:rows]

    for args in sent[None]:
        remote(*args).wait_send()

    @pl.when(active)
    def _():
        for args in sent[True]:
            remote(*args).wait_send()

    @pl.when(jnp.logical_not(active))
    def _():
        for args in sent[False]:
            remote(*args).wait_send()


def finish(row_ref, col_ref, row_out, col_out):
    row_out[...] = row_ref[...]
    col_out[...] = col_ref[...]


def per_device(dims, values, scales, reference_rows):
    A, B, N = dims
    H = A * B
    rows, width = values.shape
    refs = reference_rows.shape[0]
    pad = (rows + 15) // 16 * 16
    message = (pad, width + LANES)
    vmem = pl.BlockSpec(memory_space=pltpu.VMEM)
    dma = lambda count: pltpu.SemaphoreType.DMA((count,))
    pairs = lambda count: [dma(count), dma(count)]
    shapes = (
        jax.ShapeDtypeStruct(values.shape, BF16),
        jax.ShapeDtypeStruct(reference_rows.shape, BF16),
    )
    hbm = lambda x: pltpu.with_memory_space_constraint(x, pltpu.HBM)
    out = pl.pallas_call(
        functools.partial(kernel, dims, rows),
        out_shape=(pltpu.VMEM(values.shape, BF16), pltpu.VMEM(reference_rows.shape, BF16)),
        in_specs=[pl.BlockSpec(memory_space=pltpu.HBM)] * 3,
        out_specs=(vmem, vmem),
        scratch_shapes=[
            pltpu.VMEM(values.shape, BF16),
            pltpu.VMEM(scales.shape, F32),
            pltpu.VMEM((2,) + reference_rows.shape, BF16),
            pltpu.VMEM((H, pad, width), BF16),
            pltpu.VMEM((H, pad, width), F32),
            pltpu.VMEM((H, pad, LANES), F32),
            pltpu.VMEM((H, pad, LANES), F32),
            pltpu.VMEM((H,) + message, BF16),
            pltpu.VMEM((H,) + message, BF16),
            pltpu.VMEM((H,) + message, BF16),
            pltpu.VMEM((H,) + message, BF16),
            pltpu.VMEM((A,) + message, BF16),
            pltpu.VMEM((A,) + message, BF16),
            pltpu.VMEM((N // 2,) + message, BF16),
            pltpu.VMEM((refs, width + LANES), BF16),
            pltpu.VMEM((refs, width + LANES), BF16),
            pltpu.VMEM((pad, width), BF16),
            dma(2),
            pltpu.SemaphoreType.DMA,
            *pairs(A),
            *pairs(H),
            *pairs(H),
            *pairs(H),
            *pairs(H),
            *pairs(A),
            *pairs(N // 2),
            *pairs(3),
        ],
        compiler_params=pltpu.CompilerParams(
            collective_id=0, has_side_effects=True, vmem_limit_bytes=LIMIT
        ),
    )(hbm(values), hbm(scales), hbm(reference_rows))
    return pl.pallas_call(
        finish, out_shape=shapes, in_specs=[vmem, vmem], out_specs=(vmem, vmem),
        compiler_params=pltpu.CompilerParams(vmem_limit_bytes=LIMIT),
    )(*out)


def factors(mesh):
    wide, narrow = mesh.shape["wide"], mesh.shape["narrow"]
    assert wide % 2 == 0 and narrow % 2 == 0
    chips = wide // 2
    near = 2 if chips % 2 == 0 else 1
    return chips // near, near, narrow


def solution(mesh):
    return jax.shard_map(
        functools.partial(per_device, factors(mesh)),
        mesh=mesh,
        in_specs=(P("wide", None), P("wide", None), P(("wide", "narrow"), None)),
        out_specs=(P("wide", None), P(("wide", "narrow"), None)),
        check_vma=False,
    )
```

```python
import functools
import math

import jax
import jax.numpy as jnp
from jax import lax
from jax.experimental import pallas as pl
from jax.experimental.pallas import tpu as pltpu
from jax.sharding import PartitionSpec as P

MESH = pl.DeviceIdType.MESH
LANES = 128
LIMIT = 40 << 20
PIECES = 2
F32 = jnp.float32
BF16 = jnp.bfloat16


def split3(x):
    hi = x.astype(BF16).astype(F32)
    mid = (x - hi).astype(BF16).astype(F32)
    return hi, mid, x - hi - mid


def pack_stats(top, total):
    rows = top.shape[0]
    lane = lax.broadcasted_iota(jnp.int32, (rows, LANES), 1)
    out = jnp.zeros((rows, LANES), F32)
    for i, term in enumerate(split3(top) + split3(total)):
        out = jnp.where(lane == i, term, out)
    return out.astype(BF16)


def merge(messages, width):
    lane = lax.broadcasted_iota(jnp.int32, (messages[0].shape[0], LANES), 1)
    tops, totals = [], []
    for m in messages:
        t = m[:, width:].astype(F32)
        tops.append(jnp.sum(jnp.where(lane < 3, t, 0.0), axis=1, keepdims=True))
        totals.append(
            jnp.sum(jnp.where((lane >= 3) & (lane < 6), t, 0.0), axis=1, keepdims=True)
        )
    top = functools.reduce(jnp.maximum, tops)
    acc, total = None, None
    for m, t, s in zip(messages, tops, totals):
        shrink = jnp.exp(t - top)
        a, s = m[:, :width].astype(F32) * shrink, s * shrink
        acc, total = (a, s) if acc is None else (acc + a, total + s)
    return acc, top, total


def flip(z, i):
    bit = 1
    while bit <= i:
        if i & bit:
            z = z + bit * (1 - 2 * ((z // bit) % 2))
        bit *= 2
    return z


def kernel(
    dims, rows,
    values_hbm, scales_hbm, refs_hbm, row_out, col_out,
    values, scales, refs, q, out_r, in_r, all_g,
    load_sem, x_s, x_r, c_s, c_r, g_s, g_r, f_s, f_r, r_s, r_r, e_s, e_r,
):
    A, B, N = dims
    G = N // 2
    pad, width = q.shape[3], q.shape[4]
    count = refs.shape[1]
    factor = 1.0 / math.sqrt(width)
    w = lax.axis_index("wide")
    n = lax.axis_index("narrow")
    a, b, c = w // (B * 2), (w // 2) % B, w % 2
    g, p = n // 2, n % 2
    active = c == p
    other = 1 - p
    turn = (c + p) % 2
    source_y = (b + turn) % B

    pow2 = A & (A - 1) == 0
    to_z = [flip(a, i) if pow2 else (a + i) % A for i in range(A)]
    from_z = [flip(a, i) if pow2 else (a + A - i) % A for i in range(A)]

    def device(za, yb, core, narrow):
        return {"wide": (za * B + yb) * 2 + core, "narrow": narrow}

    cdev = device(a, b, 1 - c, n)
    xdev = device(a, b, c, g * 2 + other)
    far = [(i, j) for i in reversed(range(A)) for j in reversed(range(B)) if i or j]
    to = {(i, j): device(to_z[i], (b + j) % B, (c + j) % 2, n) for i, j in far}
    back = {(i, j): device(from_z[i], (b + j) % B, (c + j) % 2, n) for i, j in far}
    gdev = [device(a, b, c, ((g + k) % G) * 2 + p) for k in range(G)]

    mine = p * 2 + c
    load_refs = pltpu.make_async_copy(refs_hbm, refs.at[mine], load_sem.at[0])
    load_values = pltpu.make_async_copy(values_hbm, values, load_sem.at[1])
    load_scales = pltpu.make_async_copy(scales_hbm, scales, load_sem.at[2])
    load_values.start()
    load_scales.start()
    load_refs.start()

    barrier = pltpu.get_barrier_semaphore()
    partners = [back[e] for e in far] + [cdev, xdev] + gdev[1:]
    for d in partners:
        pl.semaphore_signal(barrier, inc=1, device_id=d, device_id_type=MESH)

    load_values.wait()
    load_scales.wait()
    groups = scales.shape[1]
    lane = lax.broadcasted_iota(jnp.int32, (groups, width), 1)
    group = lax.broadcasted_iota(jnp.int32, (groups, width), 0)
    spread = jnp.where(lane // (width // groups) == group, 1.0, 0.0).astype(F32)
    scale = jnp.dot(
        scales[...], spread, preferred_element_type=F32, precision=lax.Precision.HIGHEST
    )
    block = values[...].astype(F32) * scale
    if pad > rows:
        block = jnp.concatenate([block, jnp.zeros((pad - rows, width), F32)], axis=0)
    q[c, b, a] = block.astype(BF16)
    load_refs.wait()
    pl.semaphore_wait(barrier, len(partners))

    def remote(src, dst, s, r, target):
        return pltpu.make_async_remote_copy(
            src_ref=src, dst_ref=dst, send_sem=s, recv_sem=r,
            device_id=target, device_id_type=MESH,
        )

    sent = []

    def send(*args):
        remote(*args).start()
        sent.append(args)

    def arrive(dst, s, r):
        remote(dst, dst, s, r, xdev).wait_recv()

    piece = count // PIECES

    def part(slot, k):
        return refs.at[slot, k * piece : (k + 1) * piece]

    def send_queries():
        for e, (i, j) in enumerate(far):
            remote(
                q.at[c, b, a], q.at[c, b, a], g_s.at[e], g_r.at[(c * B + b) * A + a], to[i, j]
            ).start()

    def wait_queries(kind, yb, own):
        for i in range(A):
            za = from_z[i]
            r = g_r.at[(kind * B + yb) * A + za]
            if i:
                arrive(q.at[kind, yb, za], g_s.at[0], r)
            else:

                @pl.when(jnp.logical_not(own))
                def _():
                    arrive(q.at[kind, yb, za], g_s.at[0], r)

    @pl.when(active)
    def _():
        send_queries()

    for k in range(PIECES):
        send(part(mine, k), part(mine, k), x_s.at[k], x_r.at[k], xdev)
    send(refs.at[mine], refs.at[mine], c_s.at[PIECES], c_r.at[PIECES], cdev)

    wait_queries(p, source_y, active)

    @pl.when(jnp.logical_not(active))
    def _():
        send_queries()

    theirs = other * 2 + c
    for k in range(PIECES):
        arrive(part(theirs, k), x_s.at[k], x_r.at[k])
        send(part(theirs, k), part(theirs, k), c_s.at[k], c_r.at[k], cdev)
    arrive(refs.at[p * 2 + 1 - c], c_s.at[PIECES], c_r.at[PIECES])
    for k in range(PIECES):
        arrive(part(other * 2 + 1 - c, k), c_s.at[k], c_r.at[k])

    every_ref = refs[...].reshape(4 * count, width)
    block = q[p, source_y].reshape(A * pad, width)
    scores = (
        lax.dot_general(block, every_ref, (((1,), (1,)), ((), ())), preferred_element_type=F32)
        * factor
    )
    top = jnp.max(scores, axis=1, keepdims=True)
    weights = jnp.exp(scores - top)
    total = jnp.sum(weights, axis=1, keepdims=True)
    acc = jnp.dot(weights.astype(BF16), every_ref, preferred_element_type=F32)
    out_r[:, :, :width] = acc.astype(BF16).reshape(A, pad, width)
    out_r[:, :, width:] = pack_stats(top, total).reshape(A, pad, LANES)

    slot = a * B + b
    for za in range(A):
        own = active & (a == za)

        @pl.when(own)
        def _():
            in_r[slot] = out_r[za]

        @pl.when(jnp.logical_not(own))
        def _():
            remote(
                out_r.at[za], in_r.at[slot], r_s.at[2 * za], r_r.at[slot],
                device(za, source_y, p, n),
            ).start()

        send(
            out_r.at[za], in_r.at[slot], r_s.at[2 * za + 1], r_r.at[slot],
            device(za, source_y, p, g * 2 + other),
        )

    first = q.at[p, source_y]
    send(first, first, f_s.at[0], f_r.at[0], cdev)
    second_y = (b + 1 - turn) % B
    wait_queries(other, second_y, jnp.logical_not(active))
    second = q.at[other, second_y]
    send(second, second, f_s.at[1], f_r.at[1], cdev)
    arrive(q.at[p, second_y], f_s.at[0], f_r.at[0])
    arrive(q.at[other, source_y], f_s.at[1], f_r.at[1])

    every = q[...].reshape(2 * B * A * pad, width)
    scores = (
        lax.dot_general(
            refs[mine], every, (((1,), (1,)), ((), ())), preferred_element_type=F32
        )
        * factor
    )
    if pad > rows:
        column = lax.broadcasted_iota(jnp.int32, scores.shape, 1)
        scores = jnp.where(column % pad < rows, scores, -jnp.inf)
    top = jnp.max(scores, axis=1, keepdims=True)
    weights = jnp.exp(scores - top)
    total = jnp.sum(weights, axis=1, keepdims=True)
    acc = jnp.dot(weights.astype(BF16), every, preferred_element_type=F32)
    col_out[...] = (acc / total).astype(BF16)

    for za in range(A):
        for yb in range(B):
            s = za * B + yb

            @pl.when(jnp.logical_not(active & (slot == s)))
            def _():
                arrive(in_r.at[s], r_s.at[0], r_r.at[s])

    acc, top, total = merge([in_r[s] for s in range(A * B)], width)
    if G > 1:
        all_g[g, :, :width] = acc.astype(BF16)
        all_g[g, :, width:] = pack_stats(top, total)
        for k in range(1, G):
            send(all_g.at[g], all_g.at[g], e_s.at[k], e_r.at[k], gdev[k])
        for k in range(1, G):
            arrive(all_g.at[(g + G - k) % G], e_s.at[k], e_r.at[k])
        acc, top, total = merge([all_g[k] for k in range(G)], width)
    row_out[...] = (acc / total).astype(BF16)[:rows]

    for args in sent:
        remote(*args).wait_send()
    for e in range(len(far)):
        remote(q.at[c, b, a], q.at[c, b, a], g_s.at[e], g_r.at[0], xdev).wait_send()
    for za in range(A):

        @pl.when(jnp.logical_not(active & (a == za)))
        def _():
            remote(out_r.at[za], in_r.at[slot], r_s.at[2 * za], r_r.at[0], xdev).wait_send()


def finish(row_ref, col_ref, row_out, col_out):
    row_out[...] = row_ref[...]
    col_out[...] = col_ref[...]


def per_device(dims, values, scales, reference_rows):
    A, B, N = dims
    G = N // 2
    rows, width = values.shape
    pad = (rows + 15) // 16 * 16
    message = (pad, width + LANES)
    vmem = pl.BlockSpec(memory_space=pltpu.VMEM)
    dma = lambda count: pltpu.SemaphoreType.DMA((count,))
    pairs = lambda count: [dma(count), dma(count)]
    hbm = lambda x: pltpu.with_memory_space_constraint(x, pltpu.HBM)
    out = pl.pallas_call(
        functools.partial(kernel, dims, rows),
        out_shape=(pltpu.VMEM(values.shape, BF16), pltpu.VMEM(reference_rows.shape, BF16)),
        in_specs=[pl.BlockSpec(memory_space=pltpu.HBM)] * 3,
        out_specs=(vmem, vmem),
        scratch_shapes=[
            pltpu.VMEM(values.shape, BF16),
            pltpu.VMEM(scales.shape, F32),
            pltpu.VMEM((4,) + reference_rows.shape, BF16),
            pltpu.VMEM((2, B, A, pad, width), BF16),
            pltpu.VMEM((A,) + message, BF16),
            pltpu.VMEM((A * B,) + message, BF16),
            pltpu.VMEM((G,) + message, BF16),
            dma(3),
            *pairs(PIECES),
            *pairs(PIECES + 1),
            dma(A * B - 1),
            dma(2 * A * B),
            *pairs(2),
            dma(2 * A),
            dma(A * B),
            *pairs(G),
        ],
        compiler_params=pltpu.CompilerParams(
            collective_id=0, has_side_effects=True, vmem_limit_bytes=LIMIT
        ),
    )(hbm(values), hbm(scales), hbm(reference_rows))
    return pl.pallas_call(
        finish,
        out_shape=(
            jax.ShapeDtypeStruct(values.shape, BF16),
            jax.ShapeDtypeStruct(reference_rows.shape, BF16),
        ),
        in_specs=[vmem, vmem],
        out_specs=(vmem, vmem),
        compiler_params=pltpu.CompilerParams(vmem_limit_bytes=LIMIT),
    )(*out)


def factors(mesh):
    wide, narrow = mesh.shape["wide"], mesh.shape["narrow"]
    assert wide % 4 == 0 and narrow % 2 == 0
    return wide // 4, 2, narrow


def solution(mesh):
    return jax.shard_map(
        functools.partial(per_device, factors(mesh)),
        mesh=mesh,
        in_specs=(P("wide", None), P("wide", None), P(("wide", "narrow"), None)),
        out_specs=(P("wide", None), P(("wide", "narrow"), None)),
        check_vma=False,
    )
```

```python
import functools
import math

import jax
import jax.numpy as jnp
from jax import lax
from jax.experimental import pallas as pl
from jax.experimental.pallas import tpu as pltpu
from jax.sharding import PartitionSpec as P

MESH = pl.DeviceIdType.MESH
LANES = 128
LIMIT = 40 << 20
PIECES = 2
F32 = jnp.float32
BF16 = jnp.bfloat16


def split3(x):
    hi = x.astype(BF16).astype(F32)
    mid = (x - hi).astype(BF16).astype(F32)
    return hi, mid, x - hi - mid


def pack_stats(top, total):
    rows = top.shape[0]
    lane = lax.broadcasted_iota(jnp.int32, (rows, LANES), 1)
    out = jnp.zeros((rows, LANES), F32)
    for i, term in enumerate(split3(top) + split3(total)):
        out = jnp.where(lane == i, term, out)
    return out.astype(BF16)


def merge(messages, width):
    lane = lax.broadcasted_iota(jnp.int32, (messages[0].shape[0], LANES), 1)
    tops, totals = [], []
    for m in messages:
        t = m[:, width:].astype(F32)
        tops.append(jnp.sum(jnp.where(lane < 3, t, 0.0), axis=1, keepdims=True))
        totals.append(
            jnp.sum(jnp.where((lane >= 3) & (lane < 6), t, 0.0), axis=1, keepdims=True)
        )
    top = functools.reduce(jnp.maximum, tops)
    acc, total = None, None
    for m, t, s in zip(messages, tops, totals):
        shrink = jnp.exp(t - top)
        a, s = m[:, :width].astype(F32) * shrink, s * shrink
        acc, total = (a, s) if acc is None else (acc + a, total + s)
    return acc, top, total


def flip(z, i):
    bit = 1
    while bit <= i:
        if i & bit:
            z = z + bit * (1 - 2 * ((z // bit) % 2))
        bit *= 2
    return z


def kernel(
    dims, rows,
    values_hbm, scales_hbm, refs_hbm, row_out, col_out,
    values, scales, refs, q, out_r, in_r, all_g,
    load_sem, x_s, x_r, c_s, c_r, g_s, g_r, f_s, f_r, r_s, r_r, e_s, e_r,
):
    A, B, N = dims
    G = N // 2
    pad, width = q.shape[2], q.shape[3]
    count = refs.shape[1]
    factor = 1.0 / math.sqrt(width)
    w = lax.axis_index("wide")
    n = lax.axis_index("narrow")
    a, b, c = w // (B * 2), (w // 2) % B, w % 2
    g, p = n // 2, n % 2

    pow2 = A & (A - 1) == 0
    to_z = [flip(a, i) if pow2 else (a + i) % A for i in range(A)]
    from_z = [flip(a, i) if pow2 else (a + A - i) % A for i in range(A)]

    def device(za, yb, core, narrow):
        return {"wide": (za * B + yb) * 2 + core, "narrow": narrow}

    cdev = device(a, b, 1 - c, n)
    ydev = device(a, 1 - b, c, n)
    xdev = device(a, b, c, g * 2 + 1 - p)
    far = list(reversed(range(1, A)))
    gdev = [device(a, b, c, ((g + k) % G) * 2 + p) for k in range(G)]

    mine = b * 2 + c
    line = b * 2 + c
    load_refs = pltpu.make_async_copy(refs_hbm, refs.at[mine], load_sem.at[0])
    load_values = pltpu.make_async_copy(values_hbm, values, load_sem.at[1])
    load_scales = pltpu.make_async_copy(scales_hbm, scales, load_sem.at[2])
    load_values.start()
    load_scales.start()
    load_refs.start()

    barrier = pltpu.get_barrier_semaphore()
    partners = [device(from_z[i], b, c, n) for i in far] + [cdev, ydev, xdev] + gdev[1:]
    for d in partners:
        pl.semaphore_signal(barrier, inc=1, device_id=d, device_id_type=MESH)

    load_values.wait()
    load_scales.wait()
    groups = scales.shape[1]
    lane = lax.broadcasted_iota(jnp.int32, (groups, width), 1)
    group = lax.broadcasted_iota(jnp.int32, (groups, width), 0)
    spread = jnp.where(lane // (width // groups) == group, 1.0, 0.0).astype(F32)
    scale = jnp.dot(
        scales[...], spread, preferred_element_type=F32, precision=lax.Precision.HIGHEST
    )
    block = values[...].astype(F32) * scale
    if pad > rows:
        block = jnp.concatenate([block, jnp.zeros((pad - rows, width), F32)], axis=0)
    q[line, a] = block.astype(BF16)
    load_refs.wait()
    pl.semaphore_wait(barrier, len(partners))

    def remote(src, dst, s, r, target):
        return pltpu.make_async_remote_copy(
            src_ref=src, dst_ref=dst, send_sem=s, recv_sem=r,
            device_id=target, device_id_type=MESH,
        )

    sent = []

    def send(*args):
        remote(*args).start()
        sent.append(args)

    def arrive(dst, s, r):
        remote(dst, dst, s, r, xdev).wait_recv()

    piece = count // PIECES

    def part(slot, k):
        return refs.at[slot, k * piece : (k + 1) * piece]

    for i in far:
        send(q.at[line, a], q.at[line, a], g_s.at[i], g_r.at[i], device(to_z[i], b, c, n))
    for k in range(PIECES):
        send(part(mine, k), part(mine, k), x_s.at[k], x_r.at[k], ydev)
    send(refs.at[mine], refs.at[mine], c_s.at[PIECES], c_r.at[PIECES], cdev)

    for i in far:
        arrive(q.at[line, from_z[i]], g_s.at[i], g_r.at[i])
    send(q.at[line], q.at[line], f_s.at[0], f_r.at[0], cdev)

    theirs = (1 - b) * 2 + c
    for k in range(PIECES):
        arrive(part(theirs, k), x_s.at[k], x_r.at[k])
        send(part(theirs, k), part(theirs, k), c_s.at[k], c_r.at[k], cdev)
    send(q.at[line], q.at[line], f_s.at[1], f_r.at[1], ydev)
    arrive(refs.at[b * 2 + 1 - c], c_s.at[PIECES], c_r.at[PIECES])
    for k in range(PIECES):
        arrive(part((1 - b) * 2 + 1 - c, k), c_s.at[k], c_r.at[k])

    every_ref = refs[...].reshape(4 * count, width)
    block = q[line].reshape(A * pad, width)
    scores = (
        lax.dot_general(block, every_ref, (((1,), (1,)), ((), ())), preferred_element_type=F32)
        * factor
    )
    top = jnp.max(scores, axis=1, keepdims=True)
    weights = jnp.exp(scores - top)
    total = jnp.sum(weights, axis=1, keepdims=True)
    acc = jnp.dot(weights.astype(BF16), every_ref, preferred_element_type=F32)
    out_r[:, :, :width] = acc.astype(BF16).reshape(A, pad, width)
    out_r[:, :, width:] = pack_stats(top, total).reshape(A, pad, LANES)

    slot = p * A + a
    for za in range(A):

        @pl.when(a == za)
        def _():
            in_r[slot] = out_r[za]

        @pl.when(a != za)
        def _():
            remote(
                out_r.at[za], in_r.at[slot], r_s.at[2 * za], r_r.at[slot], device(za, b, c, n)
            ).start()

        send(
            out_r.at[za], in_r.at[slot], r_s.at[2 * za + 1], r_r.at[slot],
            device(za, b, c, g * 2 + 1 - p),
        )

    arrive(q.at[theirs], f_s.at[1], f_r.at[1])
    send(q.at[theirs], q.at[theirs], f_s.at[2], f_r.at[2], cdev)
    arrive(q.at[b * 2 + 1 - c], f_s.at[0], f_r.at[0])
    arrive(q.at[(1 - b) * 2 + 1 - c], f_s.at[2], f_r.at[2])

    every = q[...].reshape(2 * B * A * pad, width)
    scores = (
        lax.dot_general(
            refs[mine], every, (((1,), (1,)), ((), ())), preferred_element_type=F32
        )
        * factor
    )
    if pad > rows:
        column = lax.broadcasted_iota(jnp.int32, scores.shape, 1)
        scores = jnp.where(column % pad < rows, scores, -jnp.inf)
    top = jnp.max(scores, axis=1, keepdims=True)
    weights = jnp.exp(scores - top)
    total = jnp.sum(weights, axis=1, keepdims=True)
    acc = jnp.dot(weights.astype(BF16), every, preferred_element_type=F32)
    col_out[...] = (acc / total).astype(BF16)

    for s in range(2 * A):

        @pl.when(slot != s)
        def _():
            arrive(in_r.at[s], r_s.at[0], r_r.at[s])

    acc, top, total = merge([in_r[s] for s in range(2 * A)], width)
    if G > 1:
        all_g[g, :, :width] = acc.astype(BF16)
        all_g[g, :, width:] = pack_stats(top, total)
        for k in range(1, G):
            send(all_g.at[g], all_g.at[g], e_s.at[k], e_r.at[k], gdev[k])
        for k in range(1, G):
            arrive(all_g.at[(g + G - k) % G], e_s.at[k], e_r.at[k])
        acc, top, total = merge([all_g[k] for k in range(G)], width)
    row_out[...] = (acc / total).astype(BF16)[:rows]

    for args in sent:
        remote(*args).wait_send()
    for za in range(A):

        @pl.when(a != za)
        def _():
            remote(out_r.at[za], in_r.at[slot], r_s.at[2 * za], r_r.at[0], xdev).wait_send()


def finish(row_ref, col_ref, row_out, col_out):
    row_out[...] = row_ref[...]
    col_out[...] = col_ref[...]


def per_device(dims, values, scales, reference_rows):
    A, B, N = dims
    G = N // 2
    rows, width = values.shape
    pad = (rows + 15) // 16 * 16
    message = (pad, width + LANES)
    vmem = pl.BlockSpec(memory_space=pltpu.VMEM)
    dma = lambda count: pltpu.SemaphoreType.DMA((count,))
    pairs = lambda count: [dma(count), dma(count)]
    hbm = lambda x: pltpu.with_memory_space_constraint(x, pltpu.HBM)
    out = pl.pallas_call(
        functools.partial(kernel, dims, rows),
        out_shape=(pltpu.VMEM(values.shape, BF16), pltpu.VMEM(reference_rows.shape, BF16)),
        in_specs=[pl.BlockSpec(memory_space=pltpu.HBM)] * 3,
        out_specs=(vmem, vmem),
        scratch_shapes=[
            pltpu.VMEM(values.shape, BF16),
            pltpu.VMEM(scales.shape, F32),
            pltpu.VMEM((4,) + reference_rows.shape, BF16),
            pltpu.VMEM((2 * B, A, pad, width), BF16),
            pltpu.VMEM((A,) + message, BF16),
            pltpu.VMEM((2 * A,) + message, BF16),
            pltpu.VMEM((G,) + message, BF16),
            dma(3),
            *pairs(PIECES),
            *pairs(PIECES + 1),
            *pairs(A),
            *pairs(3),
            dma(2 * A),
            dma(2 * A),
            *pairs(G),
        ],
        compiler_params=pltpu.CompilerParams(
            collective_id=0, has_side_effects=True, vmem_limit_bytes=LIMIT
        ),
    )(hbm(values), hbm(scales), hbm(reference_rows))
    return pl.pallas_call(
        finish,
        out_shape=(
            jax.ShapeDtypeStruct(values.shape, BF16),
            jax.ShapeDtypeStruct(reference_rows.shape, BF16),
        ),
        in_specs=[vmem, vmem],
        out_specs=(vmem, vmem),
        compiler_params=pltpu.CompilerParams(vmem_limit_bytes=LIMIT),
    )(*out)


def factors(mesh):
    wide, narrow = mesh.shape["wide"], mesh.shape["narrow"]
    assert wide % 4 == 0 and narrow % 2 == 0
    return wide // 4, 2, narrow


def solution(mesh):
    return jax.shard_map(
        functools.partial(per_device, factors(mesh)),
        mesh=mesh,
        in_specs=(P("wide", None), P("wide", None), P(("wide", "narrow"), None)),
        out_specs=(P("wide", None), P(("wide", "narrow"), None)),
        check_vma=False,
    )
```
